32 devices in a mesh: ctx: 8 (over z, x), ch: 4 (over y, core).
Axes of the slice: x: 2, y: 2, z: 4, core: 2. Of those that a mesh axis runs over, the one named last changes fastest.
Arguments:
- conv_input: bfloat16 [128, 1024], P('ch', 'ctx'), may hold values from -6 to 6
- gate_value: bfloat16 [128, 1024], P('ch', 'ctx'), may hold values from -6 to 6
- out_grad: bfloat16 [128, 1024], P('ch', 'ctx'), may hold values from -6 to 6
- long_filter: bfloat16 [128, 1024], P('ch', 'ctx'), may hold values from -4 to 4
- skip_bias: float32 [128], P('ch'), may hold values from 0.5 to 1.5
- short_weight: float32 [128, 3], P('ch'), may hold values from -3.5 to 3.5
Outputs:
- input_grad: bfloat16 [128, 1024], P('ch', 'ctx')
- filter_grad: float32 [128, 1024], P('ch', 'ctx')
The draws below stay inside these ranges and needn't reach their ends.
All inputs are finite; a program needn't handle non-finite values.
Results may differ from the reference program's by a relative error of at most 0.007.
Values may be sent and summed in bfloat16 or wider, within the bound.
A program may use at most 64 MiB of HBM per device.

```python
import jax
import jax.numpy as jnp

KS = 3
FEATURE_TOTAL = 128
SEQUENCE_SPAN = 1024


def draw_long_filter(key, part):
    sampler_seeds = jax.random.split(key, 7)
    slow_share = 0.5
    delay_location = jnp.arange(SEQUENCE_SPAN, dtype=jnp.float32)[None, :]
    is_slow = jax.random.uniform(sampler_seeds[0], (FEATURE_TOTAL, 1)) < slow_share
    slow_rate = jnp.exp(jax.random.uniform(sampler_seeds[1], (FEATURE_TOTAL, 1), minval=jnp.log(0.2), maxval=jnp.log(2.0))) / SEQUENCE_SPAN
    fast_rate = jnp.exp(jax.random.uniform(sampler_seeds[2], (FEATURE_TOTAL, 1), minval=jnp.log(1.0 / 50.0), maxval=jnp.log(1.0 / 30.0)))
    rate = jnp.where(is_slow, slow_rate, fast_rate)
    spike_location = jax.random.uniform(sampler_seeds[3], (FEATURE_TOTAL, 3)) * SEQUENCE_SPAN
    spike_multiplier = jax.random.uniform(sampler_seeds[4], (FEATURE_TOTAL, 3), minval=0.5, maxval=0.8)
    damping_exponent = -rate * delay_location
    for spike_slot_number in range(3):
        damping_exponent = damping_exponent + jnp.where(delay_location > spike_location[:, spike_slot_number:spike_slot_number + 1], jnp.log(spike_multiplier[:, spike_slot_number:spike_slot_number + 1]), 0.0)
    effective = jnp.expm1(-2.0 * rate * SEQUENCE_SPAN) / jnp.expm1(-2.0 * rate)
    scale_row = effective ** (-0.5)
    rough = jnp.clip(jax.random.normal(sampler_seeds[6], (FEATURE_TOTAL, SEQUENCE_SPAN)), -4.0, 4.0)
    taps = rough * scale_row * jnp.exp(damping_exponent)
    return taps.astype(jnp.float32).astype(jnp.bfloat16)


def block_scale(own_key, extent, shards, low, top_value):
    def one(axis_at, parts):
        steps = jax.random.uniform(jax.random.fold_in(jax.random.fold_in(own_key, 6), axis_at), (parts,), jnp.float32, low / len(shards), top_value / len(shards))
        return jnp.repeat(jnp.exp(steps), extent[axis_at] // parts).reshape((-1,) + (1,) * (len(extent) - axis_at - 1))

    loudness = one(*shards[0])
    for cut in shards[1:]:
        loudness = loudness * one(*cut)
    return loudness


def noise(own_key, dims, scale, limit, pieces=(), kind=jnp.bfloat16):
    values = scale * jax.random.normal(own_key, dims, jnp.float32)
    if pieces:
        values = values * block_scale(own_key, dims, pieces, -0.22, 0.18)
    return jnp.clip(values, -limit, limit).astype(kind)


def setup_inputs(seed: int = 0) -> dict:
    key_list = jax.random.split(jax.random.key(seed), 7)
    return {
        "conv_input": noise(key_list[0], (FEATURE_TOTAL, SEQUENCE_SPAN), 1.0, 6.0, ((0, 4), (1, 8))),
        "gate_value": noise(key_list[1], (FEATURE_TOTAL, SEQUENCE_SPAN), 1.0, 6.0, ((0, 4), (1, 8))),
        "out_grad": noise(key_list[2], (FEATURE_TOTAL, SEQUENCE_SPAN), 1.0, 6.0, ((0, 4), (1, 8))),
        "long_filter": draw_long_filter(jax.random.fold_in(key_list[6], 71), 0),
        "skip_bias": jnp.clip(0.5 + 1.0 * jax.random.uniform(key_list[4], (FEATURE_TOTAL,), jnp.float32) ** block_scale(key_list[4], (FEATURE_TOTAL,), ((0, 4),), -0.2, 0.2), 0.5, 1.5),
        "short_weight": noise(key_list[5], (FEATURE_TOTAL, KS), KS ** -0.5, 3.5, ((0, 4),), jnp.float32),
    }


def reference(conv_input, gate_value, out_grad, long_filter, skip_bias, short_weight):
    conv_grad = (gate_value.astype(jnp.float32) * out_grad.astype(jnp.float32)).astype(jnp.bfloat16)
    grad_full = conv_grad.astype(jnp.float32)
    length_fft = 2 * SEQUENCE_SPAN
    spec_grad = jnp.fft.rfft(grad_full, n=length_fft, axis=1)
    spec_filter = jnp.fft.rfft(long_filter.astype(jnp.float32), n=length_fft, axis=1)
    spec_input = jnp.fft.rfft(conv_input.astype(jnp.float32), n=length_fft, axis=1)
    correlated = jnp.fft.irfft(jnp.conj(spec_filter) * spec_grad, n=length_fft, axis=1)[:, :SEQUENCE_SPAN]
    mid_grad = (correlated.astype(jnp.float32) + skip_bias[:, None] * grad_full).astype(jnp.bfloat16)
    padded = jnp.pad(mid_grad.astype(jnp.float32), ((0, 0), (0, KS - 1)))
    input_grad = jnp.zeros((FEATURE_TOTAL, SEQUENCE_SPAN), jnp.float32)
    for tap_index in range(KS):
        input_grad = input_grad + short_weight[:, tap_index:tap_index + 1] * padded[:, tap_index:tap_index + SEQUENCE_SPAN]
    lagged = jnp.fft.irfft(jnp.conj(spec_input) * spec_grad, n=length_fft, axis=1)[:, :SEQUENCE_SPAN]
    filter_grad = lagged.astype(jnp.float32) * (1.0 / (SEQUENCE_SPAN ** 0.5))
    return input_grad.astype(jnp.bfloat16), filter_grad
```

```python
import functools
import math

import jax
import jax.numpy as jnp
from jax import lax
from jax.experimental import pallas as pl
from jax.experimental.pallas import tpu as pltpu
from jax.sharding import PartitionSpec as P

LANES = 128
GROUP = 8
EARLY = 4


def gather_kernel(
    shards,
    input_ref,
    gate_ref,
    grad_ref,
    filter_ref,
    skip_ref,
    short_ref,
    input_grad_ref,
    filter_grad_ref,
    local,
    skip_row,
    short_rows,
    grads,
    pairs,
    turned,
    sums,
    halo,
    load_sem,
    grad_send,
    grad_recv,
    pair_send,
    pair_recv,
    entered,
):
    me = lax.axis_index("ctx")
    channels = local.shape[1]
    taps = short_rows.shape[0]
    groups = channels // GROUP
    bands = [slice(group * GROUP, (group + 1) * GROUP) for group in range(groups)]

    loads = [
        pltpu.make_async_copy(source, target, load_sem.at[slot])
        for slot, (source, target) in enumerate(
            (
                (gate_ref, local.at[0]),
                (grad_ref, local.at[1]),
                (filter_ref, local.at[2]),
                (input_ref, local.at[3]),
                (skip_ref, skip_row),
                (short_ref, short_rows),
            )
        )
    ]
    for load in loads:
        load.start()
    barrier = pltpu.get_barrier_semaphore()

    @pl.loop(me + 1, shards)
    def _(peer):
        pl.semaphore_signal(
            barrier, inc=1, device_id={"ctx": peer}, device_id_type=pl.DeviceIdType.MESH
        )

    @pl.when(me > 0)
    def _():
        pl.semaphore_wait(barrier, me)

    @pl.loop(0, jnp.minimum(me, shards - me))
    def _(peer):
        pl.semaphore_signal(
            entered.at[me], inc=1, device_id={"ctx": peer}, device_id_type=pl.DeviceIdType.MESH
        )

    grads[shards] = jnp.zeros((channels, LANES), jnp.bfloat16)
    pairs[0] = jnp.zeros((2 * channels, LANES), jnp.bfloat16)
    turned[1] = jnp.zeros((GROUP, 2 * channels, LANES), jnp.bfloat16)
    sums[...] = jnp.zeros_like(sums)
    halo[...] = jnp.zeros_like(halo)

    def grad_copy(source, target):
        return pltpu.make_async_remote_copy(
            src_ref=grads.at[source],
            dst_ref=grads.at[source],
            send_sem=grad_send.at[target],
            recv_sem=grad_recv.at[source],
            device_id={"ctx": target},
            device_id_type=pl.DeviceIdType.MESH,
        )

    def pair_copy(source, target):
        return pltpu.make_async_remote_copy(
            src_ref=pairs.at[source + 1],
            dst_ref=pairs.at[source + 1],
            send_sem=pair_send.at[target],
            recv_sem=pair_recv.at[source],
            device_id={"ctx": target},
            device_id_type=pl.DeviceIdType.MESH,
        )

    loads[0].wait()
    loads[1].wait()
    grads[me] = (local[0].astype(jnp.float32) * local[1].astype(jnp.float32)).astype(jnp.bfloat16)

    @pl.when(me > 0)
    def _():
        grad_copy(me, 0).start()

    loads[2].wait()
    loads[3].wait()
    taken = [local[slot].astype(jnp.float32) for slot in (2, 3)]
    pairs[me + 1] = jnp.concatenate(
        [source[at] for at in bands for source in taken], axis=0
    ).astype(jnp.bfloat16)

    @pl.loop(0, jnp.minimum(me, shards - me))
    def _(peer):
        pair_copy(me, peer).start()

    @pl.loop(1, me)
    def _(peer):
        grad_copy(me, peer).start()

    def push_up(peer):
        @pl.when(peer < shards - me)
        def _():
            pl.semaphore_wait(entered.at[peer], 1)
            pair_copy(me, peer).start()

    @pl.loop(me + 1, me + 1 + EARLY)
    def _(peer):
        push_up(peer)

    loads[4].wait()
    loads[5].wait()
    lane_row = lax.broadcasted_iota(jnp.int32, (channels, LANES), 1)
    lane = lax.broadcasted_iota(jnp.int32, (GROUP, LANES), 1)
    row = lax.broadcasted_iota(jnp.int32, (GROUP, LANES), 0)
    lane_pair = lax.broadcasted_iota(jnp.int32, (2 * channels, LANES), 1)

    wide = skip_row.shape[1]
    eye = lax.broadcasted_iota(jnp.int32, (channels, wide), 0) == lax.broadcasted_iota(
        jnp.int32, (channels, wide), 1
    )

    def column(row):
        return jnp.sum(jnp.where(eye, row, 0.0), axis=1, keepdims=True)

    skip = column(skip_row[...])
    short = [column(short_rows[tap : tap + 1, :]) for tap in range(taps)]

    def upside_down(value):
        value = pltpu.roll(value, 4, 0)
        value = jnp.where(row & 2 > 0, pltpu.roll(value, 2, 0), pltpu.roll(value, 6, 0))
        return jnp.where(row & 1 > 0, pltpu.roll(value, 1, 0), pltpu.roll(value, 7, 0))

    def step(lag, carry):
        now = me + lag

        @pl.when(lag > 0)
        def _():
            grad_copy(now, now).wait_recv()
            push_up(now + EARLY)

        @pl.when(lag != me)
        def _():
            pair_copy(lag, lag).wait_recv()

        new, old = lax.rem(lag, 2), lax.rem(lag + 1, 2)
        grad_now = grads[now].astype(jnp.float32)
        pair, before = pairs[lag + 1], pairs[lag]
        fine = [pair] + [
            pltpu.roll(jnp.where(lane_pair >= LANES - shift, before, pair), shift, 1)
            for shift in range(1, GROUP)
        ]
        kept = [turned[old, shift] for shift in range(GROUP)]
        for shift in range(GROUP):
            turned[new, shift] = fine[shift]
        for tap in range(taps - 1):
            wide_kept = kept[tap].astype(jnp.float32)
            halo[tap] += grad_now * jnp.concatenate(
                [wide_kept[2 * GROUP * group :][:GROUP] for group in range(groups)], axis=0
            )
        for group in range(groups):
            flipped = upside_down(grad_now[bands[group]])
            inside, outside = [], []
            for coarse in range(LANES // GROUP):
                reach = LANES - GROUP * coarse
                turn = flipped if coarse == 0 else pltpu.roll(flipped, reach, 1)
                inside.append(jnp.where(lane < reach, turn, 0.0))
                outside.append(jnp.where(lane < reach, 0.0, turn))
            hankel = jnp.concatenate(
                [jnp.concatenate(part, axis=0).astype(jnp.bfloat16) for part in (inside, outside)],
                axis=1,
            )
            at = slice(2 * GROUP * group, 2 * GROUP * (group + 1))
            weights = jnp.concatenate(
                [jnp.concatenate([part[at] for part in parts], axis=0) for parts in (fine, kept)],
                axis=1,
            )
            sums[group] += lax.dot_general(
                weights,
                hankel,
                (((1,), (1,)), ((), ())),
                preferred_element_type=jnp.float32,
            )
        return carry

    lax.fori_loop(0, shards - me, step, 0)

    def unfold(group, which):
        total = None
        for shift in range(GROUP):
            start = (2 * shift + which) * GROUP
            part = jnp.where(
                lane % GROUP == GROUP - 1 - row, sums[group, start : start + GROUP], 0.0
            )
            part = part if shift == 0 else pltpu.roll(part, shift, 1)
            total = part if total is None else total + part
        return pltpu.roll(total, LANES - GROUP + 1, 1, stride=1, stride_axis=0)

    own = grads[me].astype(jnp.float32)
    ahead_grad = grads[me + 1].astype(jnp.float32)

    def rounded(value):
        return value.astype(jnp.bfloat16).astype(jnp.float32)

    mid = rounded(
        jnp.concatenate([unfold(group, 0) for group in range(groups)], axis=0) + skip * own
    )
    scale = 1.0 / math.sqrt(shards * LANES)
    filter_grad_ref[...] = scale * jnp.concatenate(
        [unfold(group, 1) for group in range(groups)], axis=0
    )
    edge = [
        rounded(
            jnp.sum(halo[tap], axis=1, keepdims=True) + skip * ahead_grad[:, tap : tap + 1]
        )
        for tap in range(taps - 1)
    ]
    total = short[0] * mid
    for tap in range(1, taps):
        moved = pltpu.roll(mid, LANES - tap, 1)
        for reach in range(tap):
            moved = jnp.where(lane_row == LANES - tap + reach, edge[reach], moved)
        total = total + short[tap] * moved
    input_grad_ref[...] = total.astype(jnp.bfloat16)

    @pl.loop(0, me)
    def _(peer):
        grad_copy(me, peer).wait_send()

    @pl.loop(0, shards - me)
    def _(peer):
        @pl.when(peer != me)
        def _():
            pair_copy(me, peer).wait_send()


def place_kernel(small_ref, wide_ref, small_out, wide_out, sem):
    copies = [
        pltpu.make_async_copy(source, target, sem.at[slot])
        for slot, (source, target) in enumerate(((wide_ref, wide_out), (small_ref, small_out)))
    ]
    for copy in copies:
        copy.start()
    for copy in copies:
        copy.wait()


def placed_copy(small, wide):
    any_spec = pl.BlockSpec(memory_space=pl.ANY)
    vmem_spec = pl.BlockSpec(memory_space=pltpu.VMEM)
    return pl.pallas_call(
        place_kernel,
        out_shape=(
            jax.ShapeDtypeStruct(small.shape, small.dtype),
            jax.ShapeDtypeStruct(wide.shape, wide.dtype),
        ),
        in_specs=[vmem_spec] * 2,
        out_specs=(any_spec, any_spec),
        scratch_shapes=[pltpu.SemaphoreType.DMA((2,))],
    )(*(pltpu.with_memory_space_constraint(value, pltpu.VMEM) for value in (small, wide)))


def per_device(conv_input, gate_value, out_grad, long_filter, skip_bias, short_weight):
    channels, block_len = conv_input.shape
    taps = short_weight.shape[1]
    shards = lax.axis_size("ctx")
    any_spec = pl.BlockSpec(memory_space=pl.ANY)
    vmem_spec = pl.BlockSpec(memory_space=pltpu.VMEM)
    results = pl.pallas_call(
        functools.partial(gather_kernel, shards),
        out_shape=(
            pltpu.VMEM((channels, block_len), jnp.bfloat16),
            pltpu.VMEM((channels, block_len), jnp.float32),
        ),
        in_specs=[any_spec] * 6,
        out_specs=(vmem_spec, vmem_spec),
        scratch_shapes=[
            pltpu.VMEM((4, channels, LANES), jnp.bfloat16),
            pltpu.VMEM((1, channels), jnp.float32),
            pltpu.VMEM((taps, channels), jnp.float32),
            pltpu.VMEM((shards + 1, channels, LANES), jnp.bfloat16),
            pltpu.VMEM((shards + 1, 2 * channels, LANES), jnp.bfloat16),
            pltpu.VMEM((2, GROUP, 2 * channels, LANES), jnp.bfloat16),
            pltpu.VMEM((channels // GROUP, 2 * GROUP * GROUP, LANES), jnp.float32),
            pltpu.VMEM((taps - 1, channels, LANES), jnp.float32),
            pltpu.SemaphoreType.DMA((6,)),
            pltpu.SemaphoreType.DMA((shards,)),
            pltpu.SemaphoreType.DMA((shards,)),
            pltpu.SemaphoreType.DMA((shards,)),
            pltpu.SemaphoreType.DMA((shards,)),
            pltpu.SemaphoreType.REGULAR((shards,)),
        ],
        compiler_params=pltpu.CompilerParams(
            collective_id=0,
            has_side_effects=True,
        ),
    )(
        conv_input,
        gate_value,
        out_grad,
        long_filter,
        skip_bias.reshape(1, channels),
        short_weight.T,
    )
    return placed_copy(*results)


def solution(mesh):
    placed = (
        P("ch", "ctx"),
        P("ch", "ctx"),
        P("ch", "ctx"),
        P("ch", "ctx"),
        P("ch"),
        P("ch", None),
    )
    return jax.shard_map(
        per_device,
        mesh=mesh,
        in_specs=placed,
        out_specs=(P("ch", "ctx"), P("ch", "ctx")),
        check_vma=False,
    )
```

```python
import functools
import math

import jax
import jax.numpy as jnp
from jax import lax
from jax.experimental import pallas as pl
from jax.experimental.pallas import tpu as pltpu
from jax.sharding import PartitionSpec as P

LANES = 128
GROUP = 8
EARLY = 3


def gather_kernel(
    shards,
    input_ref,
    gate_ref,
    grad_ref,
    filter_ref,
    skip_ref,
    short_ref,
    input_grad_ref,
    filter_grad_ref,
    local,
    skip_row,
    short_rows,
    grads,
    pairs,
    rolled,
    sums,
    halo,
    load_sem,
    send_sem,
    grad_recv,
    pair_recv,
    entered,
):
    me = lax.axis_index("ctx")
    channels = local.shape[1]
    taps = short_rows.shape[0]
    groups = channels // GROUP
    bands = [slice(group * GROUP, (group + 1) * GROUP) for group in range(groups)]

    for slot, source in enumerate((gate_ref, grad_ref, filter_ref, input_ref)):
        pltpu.make_async_copy(source, local.at[slot], load_sem.at[0]).start()
    skip_load = pltpu.make_async_copy(skip_ref, skip_row, load_sem.at[1])
    short_load = pltpu.make_async_copy(short_ref, short_rows, load_sem.at[2])
    skip_load.start()
    short_load.start()
    barrier = pltpu.get_barrier_semaphore()

    @pl.loop(me + 1, shards)
    def _(peer):
        pl.semaphore_signal(
            barrier, inc=1, device_id={"ctx": peer}, device_id_type=pl.DeviceIdType.MESH
        )

    @pl.when(me > 0)
    def _():
        pl.semaphore_wait(barrier, me)

    def party(peer):
        return (peer + 1) // 2

    @pl.loop(0, jnp.minimum(me, shards - me))
    def _(peer):
        pl.semaphore_signal(
            entered.at[party(me)],
            inc=1,
            device_id={"ctx": peer},
            device_id_type=pl.DeviceIdType.MESH,
        )

    grads[shards] = jnp.zeros((channels, LANES), jnp.bfloat16)
    for spare in range(2):
        pairs[spare] = jnp.zeros((2 * channels, LANES), jnp.bfloat16)
    sums[...] = jnp.zeros_like(sums)
    halo[...] = jnp.zeros_like(halo)

    def parity(device):
        return lax.rem(shards - device, 2)

    def grad_copy(source, target):
        return pltpu.make_async_remote_copy(
            src_ref=grads.at[source],
            dst_ref=grads.at[source],
            send_sem=send_sem.at[0],
            recv_sem=grad_recv.at[(source - target - 1 + parity(target)) // 2],
            device_id={"ctx": target},
            device_id_type=pl.DeviceIdType.MESH,
        )

    def pair_copy(source, target):
        return pltpu.make_async_remote_copy(
            src_ref=pairs.at[source + 2],
            dst_ref=pairs.at[source + 2],
            send_sem=send_sem.at[1],
            recv_sem=pair_recv.at[(source + parity(target)) // 2],
            device_id={"ctx": target},
            device_id_type=pl.DeviceIdType.MESH,
        )

    pltpu.make_async_copy(local, local, load_sem.at[0]).wait()
    grads[me] = (local[0].astype(jnp.float32) * local[1].astype(jnp.float32)).astype(jnp.bfloat16)

    @pl.when(me > 0)
    def _():
        grad_copy(me, 0).start()

    taken = [local[slot].astype(jnp.float32) for slot in (2, 3)]
    pairs[me + 2] = jnp.concatenate(
        [source[band] for band in bands for source in taken], axis=0
    ).astype(jnp.bfloat16)

    @pl.when(me > 0)
    def _():
        pair_copy(me, 0).start()

    @pl.loop(1, me)
    def _(peer):
        grad_copy(me, peer).start()

        @pl.when(peer < shards - me)
        def _():
            pair_copy(me, peer).start()

    skip_load.wait()
    short_load.wait()
    lane_row = lax.broadcasted_iota(jnp.int32, (channels, LANES), 1)
    lane = lax.broadcasted_iota(jnp.int32, (GROUP, LANES), 1)
    row = lax.broadcasted_iota(jnp.int32, (GROUP, LANES), 0)
    diagonal = lane % GROUP == GROUP - 1 - row
    lane_pair = lax.broadcasted_iota(jnp.int32, (2 * channels, LANES), 1)
    span = lax.broadcasted_iota(jnp.int32, (LANES, LANES), 0) // GROUP * GROUP
    within = span + lax.broadcasted_iota(jnp.int32, (LANES, LANES), 1) < LANES

    wide = skip_row.shape[1]
    eye = lax.broadcasted_iota(jnp.int32, (channels, wide), 0) == lax.broadcasted_iota(
        jnp.int32, (channels, wide), 1
    )

    def column(value):
        return jnp.sum(jnp.where(eye, value, 0.0), axis=1, keepdims=True)

    skip = column(skip_row[...])
    short = [column(short_rows[tap : tap + 1, :]) for tap in range(taps)]

    def upside_down(value):
        value = pltpu.roll(value, 4, 0)
        value = jnp.where(row & 2 > 0, pltpu.roll(value, 2, 0), pltpu.roll(value, 6, 0))
        return jnp.where(row & 1 > 0, pltpu.roll(value, 1, 0), pltpu.roll(value, 7, 0))

    def coarse_shifts(grad):
        blocks = []
        for band in bands:
            flipped = upside_down(grad[band])
            turns = [flipped] + [
                pltpu.roll(flipped, LANES - shift, 1) for shift in range(GROUP, LANES, GROUP)
            ]
            blocks.append(jnp.concatenate(turns, axis=0).astype(jnp.bfloat16))
        return blocks

    def fine_shifts(pair, before):
        return [pair] + [
            pltpu.roll(jnp.where(lane_pair >= LANES - shift, before, pair), shift, 1)
            for shift in range(1, GROUP)
        ]

    def filter_rows(pair):
        wide_pair = pair.astype(jnp.float32)
        return jnp.concatenate(
            [wide_pair[2 * GROUP * group :][:GROUP] for group in range(groups)], axis=0
        )

    count = shards - me
    odd = parity(me)
    units = (count + odd) // 2

    def wait_for(buffer, start, size, sem):
        blocks = buffer.at[pl.ds(start, size)]
        pltpu.make_async_copy(blocks, blocks, sem).wait()

    def wait_grads(unit, final):
        lag = 2 * unit - odd + 1
        sem = grad_recv.at[unit]
        whole = 1 if final else 2

        @pl.when(lag > 0)
        def _():
            wait_for(grads, me + lag, whole, sem)

        if not final:

            @pl.when(lag == 0)
            def _():
                wait_for(grads, me + lag + 1, 1, sem)

    def wait_pairs(unit):
        lag = 2 * unit - odd
        sem = pair_recv.at[unit]
        first = jnp.logical_and(lag >= 0, lag != me)
        second = lag + 1 != me

        @pl.when(jnp.logical_and(first, second))
        def _():
            wait_for(pairs, lag + 2, 2, sem)

        @pl.when(jnp.logical_and(first, jnp.logical_not(second)))
        def _():
            wait_for(pairs, lag + 2, 1, sem)

        @pl.when(jnp.logical_and(jnp.logical_not(first), second))
        def _():
            wait_for(pairs, lag + 3, 1, sem)

    def products(unit, final):
        lag = 2 * unit - odd
        wait_grads(unit, final)
        grad = grads[me + lag + 1].astype(jnp.float32)
        middle = coarse_shifts(grad)
        after = [jnp.zeros_like(block) for block in middle]
        if not final:
            grad_after = grads[me + lag + 2].astype(jnp.float32)
            after = coarse_shifts(grad_after)
        wait_pairs(unit)
        first, second = pairs[lag + 2], pairs[lag + 3]
        early, late = fine_shifts(first, pairs[lag + 1]), fine_shifts(second, first)
        found = []
        for group in range(groups):
            hankel = jnp.concatenate(
                [
                    jnp.where(within, rolled[group], middle[group]),
                    jnp.where(within, middle[group], after[group]),
                ],
                axis=1,
            )
            at = slice(2 * GROUP * group, 2 * GROUP * (group + 1))
            weights = jnp.concatenate(
                [jnp.concatenate([part[at] for part in parts], axis=0) for parts in (early, late)],
                axis=1,
            )
            found.append(
                lax.dot_general(
                    weights,
                    hankel,
                    (((1,), (1,)), ((), ())),
                    preferred_element_type=jnp.float32,
                )
            )
            if not final:
                rolled[group] = after[group]
        for tap in range(taps - 1):
            more = grad * filter_rows(early[tap])
            if not final:
                more = more + grad_after * filter_rows(late[tap])
            halo[tap] += more
        return found

    own = grads[me].astype(jnp.float32)
    start = coarse_shifts(jnp.where(odd > 0, 0.0, own))
    for group in range(groups):
        rolled[group] = start[group]

    def push_up(wave):
        low = jnp.maximum(2 * wave - 1, me + 1)
        high = jnp.minimum(2 * wave + 1, shards - me)

        @pl.when(low < high)
        def _():
            pl.semaphore_wait(entered.at[wave], high - low)

            @pl.loop(low, high)
            def _(peer):
                pair_copy(me, peer).start()

    nearest = party(me + 1)

    @pl.loop(nearest, nearest + EARLY)
    def _(wave):
        push_up(wave)

    def step(unit, carry):
        for group, found in enumerate(products(unit, False)):
            sums[group] += found
        push_up(nearest + EARLY + unit)
        return carry

    lax.fori_loop(0, units - 1, step, 0)

    def rounded(value):
        return value.astype(jnp.bfloat16).astype(jnp.float32)

    direct = [
        skip * (own if tap == 0 else pltpu.roll(own, LANES - tap, 1)) for tap in range(taps)
    ]
    totals = [sums[group] + found for group, found in enumerate(products(units - 1, True))]
    ahead_grad = grads[me + 1].astype(jnp.float32)
    edge = [
        rounded(jnp.sum(halo[tap], axis=1, keepdims=True) + skip * ahead_grad[:, tap : tap + 1])
        for tap in range(taps - 1)
    ]

    def folded(group, which):
        parts = []
        for shift in range(GROUP):
            at = (2 * shift + which) * GROUP
            part = jnp.where(diagonal, totals[group][at : at + GROUP], 0.0)
            parts.append(part if shift == 0 else pltpu.roll(part, shift, 1))
        while len(parts) > 1:
            parts = [left + right for left, right in zip(parts[::2], parts[1::2])]
        return parts[0]

    def straight(values, ahead):
        return jnp.concatenate(
            [
                pltpu.roll(value, LANES - GROUP + 1 - ahead, 1, stride=1, stride_axis=0)
                for value in values
            ],
            axis=0,
        )

    middles = [folded(group, 0) for group in range(groups)]
    total = None
    for tap in range(taps):
        moved = rounded(straight(middles, tap) + direct[tap])
        for reach in range(tap):
            moved = jnp.where(lane_row == LANES - tap + reach, edge[reach], moved)
        total = short[tap] * moved if total is None else total + short[tap] * moved
    input_grad_ref[...] = total.astype(jnp.bfloat16)
    scale = 1.0 / math.sqrt(shards * LANES)
    filter_grad_ref[...] = scale * straight([folded(group, 1) for group in range(groups)], 0)

    @pl.loop(0, me)
    def _(peer):
        grad_copy(me, peer).wait_send()

    @pl.loop(0, shards - me)
    def _(peer):
        @pl.when(peer != me)
        def _():
            pair_copy(me, peer).wait_send()


def place_kernel(small_ref, wide_ref, small_out, wide_out, sem):
    copies = [
        pltpu.make_async_copy(source, target, sem.at[slot])
        for slot, (source, target) in enumerate(((wide_ref, wide_out), (small_ref, small_out)))
    ]
    for copy in copies:
        copy.start()
    for copy in copies:
        copy.wait()


def placed_copy(small, wide):
    any_spec = pl.BlockSpec(memory_space=pl.ANY)
    vmem_spec = pl.BlockSpec(memory_space=pltpu.VMEM)
    return pl.pallas_call(
        place_kernel,
        out_shape=(
            jax.ShapeDtypeStruct(small.shape, small.dtype),
            jax.ShapeDtypeStruct(wide.shape, wide.dtype),
        ),
        in_specs=[vmem_spec] * 2,
        out_specs=(any_spec, any_spec),
        scratch_shapes=[pltpu.SemaphoreType.DMA((2,))],
    )(*(pltpu.with_memory_space_constraint(value, pltpu.VMEM) for value in (small, wide)))


def per_device(conv_input, gate_value, out_grad, long_filter, skip_bias, short_weight):
    channels, block_len = conv_input.shape
    taps = short_weight.shape[1]
    shards = lax.axis_size("ctx")
    any_spec = pl.BlockSpec(memory_space=pl.ANY)
    vmem_spec = pl.BlockSpec(memory_space=pltpu.VMEM)
    results = pl.pallas_call(
        functools.partial(gather_kernel, shards),
        out_shape=(
            pltpu.VMEM((channels, block_len), jnp.bfloat16),
            pltpu.VMEM((channels, block_len), jnp.float32),
        ),
        in_specs=[any_spec] * 6,
        out_specs=(vmem_spec, vmem_spec),
        scratch_shapes=[
            pltpu.VMEM((4, channels, LANES), jnp.bfloat16),
            pltpu.VMEM((1, channels), jnp.float32),
            pltpu.VMEM((taps, channels), jnp.float32),
            pltpu.VMEM((shards + 1, channels, LANES), jnp.bfloat16),
            pltpu.VMEM((shards + 2, 2 * channels, LANES), jnp.bfloat16),
            pltpu.VMEM((channels // GROUP, LANES, LANES), jnp.bfloat16),
            pltpu.VMEM((channels // GROUP, 2 * GROUP * GROUP, LANES), jnp.float32),
            pltpu.VMEM((taps - 1, channels, LANES), jnp.float32),
            pltpu.SemaphoreType.DMA((3,)),
            pltpu.SemaphoreType.DMA((2,)),
            pltpu.SemaphoreType.DMA(((shards + 1) // 2,)),
            pltpu.SemaphoreType.DMA(((shards + 1) // 2,)),
            pltpu.SemaphoreType.REGULAR((shards // 2 + 1,)),
        ],
        compiler_params=pltpu.CompilerParams(
            collective_id=0,
            has_side_effects=True,
        ),
    )(
        conv_input,
        gate_value,
        out_grad,
        long_filter,
        skip_bias.reshape(1, channels),
        short_weight.T,
    )
    return placed_copy(*results)


def solution(mesh):
    placed = (
        P("ch", "ctx"),
        P("ch", "ctx"),
        P("ch", "ctx"),
        P("ch", "ctx"),
        P("ch"),
        P("ch", None),
    )
    return jax.shard_map(
        per_device,
        mesh=mesh,
        in_specs=placed,
        out_specs=(P("ch", "ctx"), P("ch", "ctx")),
        check_vma=False,
    )
```

```python
import functools
import math

import jax
import jax.numpy as jnp
from jax import lax
from jax.experimental import pallas as pl
from jax.experimental.pallas import tpu as pltpu
from jax.sharding import PartitionSpec as P

LANES = 128
GROUP = 8
EARLY = 3


def gather_kernel(
    shards,
    input_ref,
    gate_ref,
    grad_ref,
    filter_ref,
    skip_ref,
    short_ref,
    input_grad_ref,
    filter_grad_ref,
    local,
    skip_row,
    short_rows,
    grads,
    pairs,
    rolled,
    sums,
    halo,
    load_sem,
    send_sem,
    grad_recv,
    pair_recv,
    entered,
):
    me = lax.axis_index("ctx")
    channels = local.shape[1]
    taps = short_rows.shape[0]
    groups = channels // GROUP
    bands = [slice(group * GROUP, (group + 1) * GROUP) for group in range(groups)]

    for slot, source in enumerate((gate_ref, grad_ref, filter_ref, input_ref)):
        pltpu.make_async_copy(source, local.at[slot], load_sem.at[slot // 2]).start()
    skip_load = pltpu.make_async_copy(skip_ref, skip_row, load_sem.at[0])
    short_load = pltpu.make_async_copy(short_ref, short_rows, load_sem.at[1])
    barrier = pltpu.get_barrier_semaphore()

    @pl.loop(me + 1, shards)
    def _(peer):
        pl.semaphore_signal(
            barrier, inc=1, device_id={"ctx": peer}, device_id_type=pl.DeviceIdType.MESH
        )

    @pl.when(me > 0)
    def _():
        pl.semaphore_wait(barrier, me)

    def party(peer):
        return (peer + 1) // 2

    @pl.loop(0, jnp.minimum(me, shards - me))
    def _(peer):
        pl.semaphore_signal(
            entered.at[party(me) - 1],
            inc=1,
            device_id={"ctx": peer},
            device_id_type=pl.DeviceIdType.MESH,
        )

    grads[shards] = jnp.zeros((channels, LANES), jnp.bfloat16)
    for spare in range(2):
        pairs[spare] = jnp.zeros((2 * channels, LANES), jnp.bfloat16)
    sums[...] = jnp.zeros_like(sums)
    halo[...] = jnp.zeros_like(halo)

    def parity(device):
        return lax.rem(shards - device, 2)

    def grad_copy(source, target):
        return pltpu.make_async_remote_copy(
            src_ref=grads.at[source],
            dst_ref=grads.at[source],
            send_sem=send_sem,
            recv_sem=grad_recv.at[(source - target - 1 + parity(target)) // 2],
            device_id={"ctx": target},
            device_id_type=pl.DeviceIdType.MESH,
        )

    def pair_copy(source, target):
        return pltpu.make_async_remote_copy(
            src_ref=pairs.at[source + 2],
            dst_ref=pairs.at[source + 2],
            send_sem=send_sem,
            recv_sem=pair_recv.at[(source + parity(target)) // 2],
            device_id={"ctx": target},
            device_id_type=pl.DeviceIdType.MESH,
        )

    def wait_loads(half):
        blocks = local.at[pl.ds(2 * half, 2)]
        pltpu.make_async_copy(blocks, blocks, load_sem.at[half]).wait()

    wait_loads(0)
    grads[me] = (local[0].astype(jnp.float32) * local[1].astype(jnp.float32)).astype(jnp.bfloat16)

    @pl.when(me > 0)
    def _():
        grad_copy(me, 0).start()

    wait_loads(1)
    taken = [local[slot].astype(jnp.float32) for slot in (2, 3)]
    pairs[me + 2] = jnp.concatenate(
        [source[band] for band in bands for source in taken], axis=0
    ).astype(jnp.bfloat16)

    @pl.when(me > 0)
    def _():
        pair_copy(me, 0).start()

    @pl.loop(1, me)
    def _(peer):
        grad_copy(me, peer).start()

        @pl.when(peer < shards - me)
        def _():
            pair_copy(me, peer).start()

    skip_load.start()
    short_load.start()
    lane_row = lax.broadcasted_iota(jnp.int32, (channels, LANES), 1)
    lane = lax.broadcasted_iota(jnp.int32, (GROUP, LANES), 1)
    row = lax.broadcasted_iota(jnp.int32, (GROUP, LANES), 0)
    diagonal = lane % GROUP == GROUP - 1 - row
    lane_pair = lax.broadcasted_iota(jnp.int32, (2 * channels, LANES), 1)
    span = lax.broadcasted_iota(jnp.int32, (LANES, LANES), 0) // GROUP * GROUP
    within = span + lax.broadcasted_iota(jnp.int32, (LANES, LANES), 1) < LANES

    def upside_down(value):
        value = pltpu.roll(value, 4, 0)
        value = jnp.where(row & 2 > 0, pltpu.roll(value, 2, 0), pltpu.roll(value, 6, 0))
        return jnp.where(row & 1 > 0, pltpu.roll(value, 1, 0), pltpu.roll(value, 7, 0))

    def coarse_shifts(grad):
        blocks = []
        for band in bands:
            flipped = upside_down(grad[band])
            turns = [flipped] + [
                pltpu.roll(flipped, LANES - shift, 1) for shift in range(GROUP, LANES, GROUP)
            ]
            blocks.append(jnp.concatenate(turns, axis=0).astype(jnp.bfloat16))
        return blocks

    def fine_shifts(pair, before):
        return [pair] + [
            pltpu.roll(jnp.where(lane_pair >= LANES - shift, before, pair), shift, 1)
            for shift in range(1, GROUP)
        ]

    def filter_rows(pair):
        wide_pair = pair.astype(jnp.float32)
        return jnp.concatenate(
            [wide_pair[2 * GROUP * group :][:GROUP] for group in range(groups)], axis=0
        )

    count = shards - me
    odd = parity(me)
    units = (count + odd) // 2

    def wait_for(buffer, start, size, sem):
        blocks = buffer.at[pl.ds(start, size)]
        pltpu.make_async_copy(blocks, blocks, sem).wait()

    def wait_grads(unit, final):
        lag = 2 * unit - odd + 1
        sem = grad_recv.at[unit]
        whole = 1 if final else 2

        @pl.when(lag > 0)
        def _():
            wait_for(grads, me + lag, whole, sem)

        if not final:

            @pl.when(lag == 0)
            def _():
                wait_for(grads, me + lag + 1, 1, sem)

    def wait_pairs(unit):
        lag = 2 * unit - odd
        sem = pair_recv.at[unit]
        first = jnp.logical_and(lag >= 0, lag != me)
        second = lag + 1 != me

        @pl.when(jnp.logical_and(first, second))
        def _():
            wait_for(pairs, lag + 2, 2, sem)

        @pl.when(jnp.logical_and(first, jnp.logical_not(second)))
        def _():
            wait_for(pairs, lag + 2, 1, sem)

        @pl.when(jnp.logical_and(jnp.logical_not(first), second))
        def _():
            wait_for(pairs, lag + 3, 1, sem)

    def products(unit, final):
        lag = 2 * unit - odd
        wait_grads(unit, final)
        grad = grads[me + lag + 1].astype(jnp.float32)
        middle = coarse_shifts(grad)
        after = [jnp.zeros_like(block) for block in middle]
        if not final:
            grad_after = grads[me + lag + 2].astype(jnp.float32)
            after = coarse_shifts(grad_after)
        wait_pairs(unit)
        first, second = pairs[lag + 2], pairs[lag + 3]
        early, late = fine_shifts(first, pairs[lag + 1]), fine_shifts(second, first)
        found = []
        for group in range(groups):
            hankel = jnp.concatenate(
                [
                    jnp.where(within, rolled[group], middle[group]),
                    jnp.where(within, middle[group], after[group]),
                ],
                axis=1,
            )
            at = slice(2 * GROUP * group, 2 * GROUP * (group + 1))
            weights = jnp.concatenate(
                [jnp.concatenate([part[at] for part in parts], axis=0) for parts in (early, late)],
                axis=1,
            )
            found.append(
                lax.dot_general(
                    weights,
                    hankel,
                    (((1,), (1,)), ((), ())),
                    preferred_element_type=jnp.float32,
                )
            )
            if not final:
                rolled[group] = after[group]
        for tap in range(taps - 1):
            more = grad * filter_rows(early[tap])
            if not final:
                more = more + grad_after * filter_rows(late[tap])
            halo[tap] += more
        return found

    own = grads[me].astype(jnp.float32)
    start = coarse_shifts(jnp.where(odd > 0, 0.0, own))
    for group in range(groups):
        rolled[group] = start[group]

    def push_up(wave):
        low = jnp.maximum(2 * wave - 1, me + 1)
        high = jnp.minimum(2 * wave + 1, shards - me)

        @pl.when(low < high)
        def _():
            pl.semaphore_wait(entered.at[wave - 1], high - low)

            @pl.loop(low, high)
            def _(peer):
                pair_copy(me, peer).start()

    nearest = party(me + 1)

    @pl.loop(nearest, nearest + EARLY)
    def _(wave):
        push_up(wave)

    skip_load.wait()
    short_load.wait()
    wide = skip_row.shape[1]
    eye = lax.broadcasted_iota(jnp.int32, (channels, wide), 0) == lax.broadcasted_iota(
        jnp.int32, (channels, wide), 1
    )

    def column(value):
        return jnp.sum(jnp.where(eye, value, 0.0), axis=1, keepdims=True)

    skip = column(skip_row[...])
    short = [column(short_rows[tap : tap + 1, :]) for tap in range(taps)]

    def step(unit, carry):
        for group, found in enumerate(products(unit, False)):
            sums[group] += found
        push_up(nearest + EARLY + unit)
        return carry

    lax.fori_loop(0, units - 1, step, 0)

    def rounded(value):
        return value.astype(jnp.bfloat16).astype(jnp.float32)

    direct = [
        skip * (own if tap == 0 else pltpu.roll(own, LANES - tap, 1)) for tap in range(taps)
    ]
    sent = shards - me - jnp.where(2 * me < shards, 1, 0)

    @pl.loop(0, me)
    def _(peer):
        grad_copy(me, peer).wait_send()

    @pl.loop(1, sent)
    def _(peer):
        pair_copy(me, lax.rem(me + 1, shards)).wait_send()

    totals = [sums[group] + found for group, found in enumerate(products(units - 1, True))]
    ahead_grad = grads[me + 1].astype(jnp.float32)
    edge = [
        rounded(jnp.sum(halo[tap], axis=1, keepdims=True) + skip * ahead_grad[:, tap : tap + 1])
        for tap in range(taps - 1)
    ]

    def folded(group, which):
        parts = []
        for shift in range(GROUP):
            at = (2 * shift + which) * GROUP
            part = jnp.where(diagonal, totals[group][at : at + GROUP], 0.0)
            parts.append(part if shift == 0 else pltpu.roll(part, shift, 1))
        while len(parts) > 1:
            parts = [left + right for left, right in zip(parts[::2], parts[1::2])]
        return parts[0]

    def straight(values, ahead):
        return jnp.concatenate(
            [
                pltpu.roll(value, LANES - GROUP + 1 - ahead, 1, stride=1, stride_axis=0)
                for value in values
            ],
            axis=0,
        )

    middles = [folded(group, 0) for group in range(groups)]
    total = None
    for tap in range(taps):
        moved = rounded(straight(middles, tap) + direct[tap])
        for reach in range(tap):
            moved = jnp.where(lane_row == LANES - tap + reach, edge[reach], moved)
        total = short[tap] * moved if total is None else total + short[tap] * moved
    input_grad_ref[...] = total.astype(jnp.bfloat16)
    scale = 1.0 / math.sqrt(shards * LANES)
    filter_grad_ref[...] = scale * straight([folded(group, 1) for group in range(groups)], 0)

    @pl.when(sent > 0)
    def _():
        pair_copy(me, lax.rem(me + 1, shards)).wait_send()


def place_kernel(small_ref, wide_ref, small_out, wide_out, sem):
    copies = [
        pltpu.make_async_copy(source, target, sem.at[slot])
        for slot, (source, target) in enumerate(((wide_ref, wide_out), (small_ref, small_out)))
    ]
    for copy in copies:
        copy.start()
    for copy in copies:
        copy.wait()


def placed_copy(small, wide):
    any_spec = pl.BlockSpec(memory_space=pl.ANY)
    vmem_spec = pl.BlockSpec(memory_space=pltpu.VMEM)
    return pl.pallas_call(
        place_kernel,
        out_shape=(
            jax.ShapeDtypeStruct(small.shape, small.dtype),
            jax.ShapeDtypeStruct(wide.shape, wide.dtype),
        ),
        in_specs=[vmem_spec] * 2,
        out_specs=(any_spec, any_spec),
        scratch_shapes=[pltpu.SemaphoreType.DMA((2,))],
    )(*(pltpu.with_memory_space_constraint(value, pltpu.VMEM) for value in (small, wide)))


def per_device(conv_input, gate_value, out_grad, long_filter, skip_bias, short_weight):
    channels, block_len = conv_input.shape
    taps = short_weight.shape[1]
    shards = lax.axis_size("ctx")
    any_spec = pl.BlockSpec(memory_space=pl.ANY)
    vmem_spec = pl.BlockSpec(memory_space=pltpu.VMEM)
    results = pl.pallas_call(
        functools.partial(gather_kernel, shards),
        out_shape=(
            pltpu.VMEM((channels, block_len), jnp.bfloat16),
            pltpu.VMEM((channels, block_len), jnp.float32),
        ),
        in_specs=[any_spec] * 6,
        out_specs=(vmem_spec, vmem_spec),
        scratch_shapes=[
            pltpu.VMEM((4, channels, LANES), jnp.bfloat16),
            pltpu.VMEM((1, channels), jnp.float32),
            pltpu.VMEM((taps, channels), jnp.float32),
            pltpu.VMEM((shards + 1, channels, LANES), jnp.bfloat16),
            pltpu.VMEM((shards + 2, 2 * channels, LANES), jnp.bfloat16),
            pltpu.VMEM((channels // GROUP, LANES, LANES), jnp.bfloat16),
            pltpu.VMEM((channels // GROUP, 2 * GROUP * GROUP, LANES), jnp.float32),
            pltpu.VMEM((taps - 1, channels, LANES), jnp.float32),
            pltpu.SemaphoreType.DMA((2,)),
            pltpu.SemaphoreType.DMA,
            pltpu.SemaphoreType.DMA(((shards + 1) // 2,)),
            pltpu.SemaphoreType.DMA(((shards + 1) // 2,)),
            pltpu.SemaphoreType.REGULAR((shards // 2,)),
        ],
        compiler_params=pltpu.CompilerParams(
            collective_id=0,
            has_side_effects=True,
        ),
    )(
        conv_input,
        gate_value,
        out_grad,
        long_filter,
        skip_bias.reshape(1, channels),
        short_weight.T,
    )
    return placed_copy(*results)


def solution(mesh):
    placed = (
        P("ch", "ctx"),
        P("ch", "ctx"),
        P("ch", "ctx"),
        P("ch", "ctx"),
        P("ch"),
        P("ch", None),
    )
    return jax.shard_map(
        per_device,
        mesh=mesh,
        in_specs=placed,
        out_specs=(P("ch", "ctx"), P("ch", "ctx")),
        check_vma=False,
    )
```

```python
import functools
import math

import jax
import jax.numpy as jnp
from jax import lax
from jax.experimental import pallas as pl
from jax.experimental.pallas import tpu as pltpu
from jax.sharding import PartitionSpec as P

LANES = 128
GROUP = 8
EARLY = 3
PAD = 4


def gather_kernel(
    shards,
    input_ref,
    gate_ref,
    grad_ref,
    filter_ref,
    skip_ref,
    short_ref,
    input_grad_ref,
    filter_grad_ref,
    local,
    skip_row,
    short_rows,
    grads,
    pairs,
    rolled,
    sums,
    halo,
    load_sem,
    send_sem,
    grad_recv,
    pair_recv,
    entered,
):
    me = lax.axis_index("ctx")
    channels = local.shape[1]
    taps = short_rows.shape[0]
    groups = channels // GROUP
    bands = [slice(group * GROUP, (group + 1) * GROUP) for group in range(groups)]

    for slot, source in enumerate((gate_ref, grad_ref, filter_ref, input_ref)):
        pltpu.make_async_copy(source, local.at[slot], load_sem.at[slot // 2]).start()
    skip_load = pltpu.make_async_copy(skip_ref, skip_row, load_sem.at[0])
    short_load = pltpu.make_async_copy(short_ref, short_rows, load_sem.at[1])
    barrier = pltpu.get_barrier_semaphore()

    @pl.loop(me + 1, shards)
    def _(peer):
        pl.semaphore_signal(
            barrier, inc=1, device_id={"ctx": peer}, device_id_type=pl.DeviceIdType.MESH
        )

    @pl.when(me > 0)
    def _():
        pl.semaphore_wait(barrier, me)

    def party(peer):
        return (peer + 1) // 2

    @pl.loop(0, jnp.minimum(me, shards - me))
    def _(peer):
        pl.semaphore_signal(
            entered.at[party(me) - 1],
            inc=1,
            device_id={"ctx": peer},
            device_id_type=pl.DeviceIdType.MESH,
        )

    grads[shards] = jnp.zeros((channels, LANES), jnp.bfloat16)
    for spare in range(PAD):
        pairs[spare] = jnp.zeros((2 * channels, LANES), jnp.bfloat16)
    sums[...] = jnp.zeros_like(sums)
    halo[...] = jnp.zeros_like(halo)

    def parity(device):
        return lax.rem(shards - device, 2)

    def grad_copy(source, target):
        return pltpu.make_async_remote_copy(
            src_ref=grads.at[source],
            dst_ref=grads.at[source],
            send_sem=send_sem,
            recv_sem=grad_recv.at[(source - target - 1 + parity(target)) // 2],
            device_id={"ctx": target},
            device_id_type=pl.DeviceIdType.MESH,
        )

    def pair_copy(source, target):
        return pltpu.make_async_remote_copy(
            src_ref=pairs.at[source + PAD],
            dst_ref=pairs.at[source + PAD],
            send_sem=send_sem,
            recv_sem=pair_recv.at[(source + parity(target)) // 2],
            device_id={"ctx": target},
            device_id_type=pl.DeviceIdType.MESH,
        )

    def wait_loads(half):
        blocks = local.at[pl.ds(2 * half, 2)]
        pltpu.make_async_copy(blocks, blocks, load_sem.at[half]).wait()

    wait_loads(0)
    grads[me] = (local[0].astype(jnp.float32) * local[1].astype(jnp.float32)).astype(jnp.bfloat16)

    @pl.when(me > 0)
    def _():
        grad_copy(me, 0).start()

    wait_loads(1)
    taken = [local[slot].astype(jnp.float32) for slot in (2, 3)]
    pairs[me + PAD] = jnp.concatenate(
        [source[band] for band in bands for source in taken], axis=0
    ).astype(jnp.bfloat16)

    @pl.when(me > 0)
    def _():
        pair_copy(me, 0).start()

    @pl.loop(1, me)
    def _(peer):
        grad_copy(me, peer).start()

        @pl.when(peer < shards - me)
        def _():
            pair_copy(me, peer).start()

    skip_load.start()
    short_load.start()
    lane_row = lax.broadcasted_iota(jnp.int32, (channels, LANES), 1)
    lane = lax.broadcasted_iota(jnp.int32, (GROUP, LANES), 1)
    row = lax.broadcasted_iota(jnp.int32, (GROUP, LANES), 0)
    diagonal = lane % GROUP == GROUP - 1 - row
    lane_pair = lax.broadcasted_iota(jnp.int32, (2 * channels, LANES), 1)
    span = lax.broadcasted_iota(jnp.int32, (LANES, LANES), 0) // GROUP * GROUP
    within = span + lax.broadcasted_iota(jnp.int32, (LANES, LANES), 1) < LANES

    def upside_down(value):
        value = pltpu.roll(value, 4, 0)
        value = jnp.where(row & 2 > 0, pltpu.roll(value, 2, 0), pltpu.roll(value, 6, 0))
        return jnp.where(row & 1 > 0, pltpu.roll(value, 1, 0), pltpu.roll(value, 7, 0))

    def coarse_shifts(grad):
        blocks = []
        for band in bands:
            flipped = upside_down(grad[band])
            turns = [flipped] + [
                pltpu.roll(flipped, LANES - shift, 1) for shift in range(GROUP, LANES, GROUP)
            ]
            blocks.append(jnp.concatenate(turns, axis=0).astype(jnp.bfloat16))
        return blocks

    def fine_shifts(pair, before):
        return [pair] + [
            pltpu.roll(jnp.where(lane_pair >= LANES - shift, before, pair), shift, 1)
            for shift in range(1, GROUP)
        ]

    def filter_rows(pair):
        wide_pair = pair.astype(jnp.float32)
        return jnp.concatenate(
            [wide_pair[2 * GROUP * group :][:GROUP] for group in range(groups)], axis=0
        )

    count = shards - me
    odd = parity(me)
    units = (count + odd) // 2

    def wait_for(buffer, start, size, sem):
        blocks = buffer.at[pl.ds(start, size)]
        pltpu.make_async_copy(blocks, blocks, sem).wait()

    def wait_grads(unit, final):
        lag = 2 * unit - odd + 1
        sem = grad_recv.at[unit]
        whole = 1 if final else 2

        @pl.when(lag > 0)
        def _():
            wait_for(grads, me + lag, whole, sem)

        if not final:

            @pl.when(lag == 0)
            def _():
                wait_for(grads, me + lag + 1, 1, sem)

    def wait_pairs(unit):
        lag = 2 * unit - odd
        sem = pair_recv.at[unit]
        first = jnp.logical_and(lag >= 0, lag != me)
        second = jnp.logical_and(lag >= -1, lag + 1 != me)

        @pl.when(jnp.logical_and(first, second))
        def _():
            wait_for(pairs, lag + PAD, 2, sem)

        @pl.when(jnp.logical_and(first, jnp.logical_not(second)))
        def _():
            wait_for(pairs, lag + PAD, 1, sem)

        @pl.when(jnp.logical_and(jnp.logical_not(first), second))
        def _():
            wait_for(pairs, lag + PAD + 1, 1, sem)

    def products(unit, final):
        lag = 2 * unit - odd
        width = 4 if final else 2
        wait_grads(unit, False)
        if final:
            wait_grads(unit + 1, True)
        known = []
        for ahead in range(1, width + (not final)):
            at = lag + ahead
            grad = grads[jnp.maximum(me + at, 0)].astype(jnp.float32)
            known.append(jnp.where(at < 0, 0.0, grad) if final else grad)
        turns = [None] + [coarse_shifts(grad) for grad in known]
        wait_pairs(unit)
        if final:
            wait_pairs(unit + 1)
        blocks = [pairs[lag + PAD + ahead] for ahead in range(-1, width)]
        rows = [fine_shifts(new, old) for old, new in zip(blocks, blocks[1:])]
        found = []
        for group in range(groups):
            stack = [rolled[group]] + [turn[group] for turn in turns[1:]]
            if final:
                stack.append(jnp.zeros_like(stack[0]))
            hankel = jnp.concatenate(
                [jnp.where(within, old, new) for old, new in zip(stack, stack[1:])], axis=1
            )
            at = slice(2 * GROUP * group, 2 * GROUP * (group + 1))
            weights = jnp.concatenate(
                [jnp.concatenate([part[at] for part in parts], axis=0) for parts in rows],
                axis=1,
            )
            found.append(
                lax.dot_general(
                    weights,
                    hankel,
                    (((1,), (1,)), ((), ())),
                    preferred_element_type=jnp.float32,
                )
            )
            if not final:
                rolled[group] = stack[-1]
        for tap in range(taps - 1):
            more = None
            for grad, parts in zip(known, rows):
                term = grad * filter_rows(parts[tap])
                more = term if more is None else more + term
            halo[tap] += more
        return found

    own = grads[me].astype(jnp.float32)
    start = coarse_shifts(jnp.where(odd > 0, 0.0, own))
    for group in range(groups):
        rolled[group] = start[group]

    def push_up(wave):
        low = jnp.maximum(2 * wave - 1, me + 1)
        high = jnp.minimum(2 * wave + 1, shards - me)

        @pl.when(low < high)
        def _():
            pl.semaphore_wait(entered.at[wave - 1], high - low)

            @pl.loop(low, high)
            def _(peer):
                pair_copy(me, peer).start()

    nearest = party(me + 1)

    @pl.loop(nearest, nearest + EARLY)
    def _(wave):
        push_up(wave)

    skip_load.wait()
    short_load.wait()
    wide = skip_row.shape[1]
    eye = lax.broadcasted_iota(jnp.int32, (channels, wide), 0) == lax.broadcasted_iota(
        jnp.int32, (channels, wide), 1
    )

    def column(value):
        return jnp.sum(jnp.where(eye, value, 0.0), axis=1, keepdims=True)

    skip = column(skip_row[...])
    short = [column(short_rows[tap : tap + 1, :]) for tap in range(taps)]

    def step(unit, carry):
        for group, found in enumerate(products(unit, False)):
            sums[group] += found
        push_up(nearest + EARLY + unit)
        return carry

    lax.fori_loop(0, units - 2, step, 0)

    def rounded(value):
        return value.astype(jnp.bfloat16).astype(jnp.float32)

    direct = [
        skip * (own if tap == 0 else pltpu.roll(own, LANES - tap, 1)) for tap in range(taps)
    ]
    sent = shards - me - jnp.where(2 * me < shards, 1, 0)

    @pl.loop(0, me)
    def _(peer):
        grad_copy(me, peer).wait_send()

    @pl.loop(1, sent)
    def _(peer):
        pair_copy(me, lax.rem(me + 1, shards)).wait_send()

    totals = [sums[group] + found for group, found in enumerate(products(units - 2, True))]
    ahead_grad = grads[me + 1].astype(jnp.float32)
    edge = [
        rounded(jnp.sum(halo[tap], axis=1, keepdims=True) + skip * ahead_grad[:, tap : tap + 1])
        for tap in range(taps - 1)
    ]

    def folded(group, which):
        parts = []
        for shift in range(GROUP):
            at = (2 * shift + which) * GROUP
            part = jnp.where(diagonal, totals[group][at : at + GROUP], 0.0)
            parts.append(part if shift == 0 else pltpu.roll(part, shift, 1))
        while len(parts) > 1:
            parts = [left + right for left, right in zip(parts[::2], parts[1::2])]
        return parts[0]

    def straight(values, ahead):
        return jnp.concatenate(
            [
                pltpu.roll(value, LANES - GROUP + 1 - ahead, 1, stride=1, stride_axis=0)
                for value in values
            ],
            axis=0,
        )

    middles = [folded(group, 0) for group in range(groups)]
    total = None
    for tap in range(taps):
        moved = rounded(straight(middles, tap) + direct[tap])
        for reach in range(tap):
            moved = jnp.where(lane_row == LANES - tap + reach, edge[reach], moved)
        total = short[tap] * moved if total is None else total + short[tap] * moved
    input_grad_ref[...] = total.astype(jnp.bfloat16)
    scale = 1.0 / math.sqrt(shards * LANES)
    filter_grad_ref[...] = scale * straight([folded(group, 1) for group in range(groups)], 0)

    @pl.when(sent > 0)
    def _():
        pair_copy(me, lax.rem(me + 1, shards)).wait_send()


def place_kernel(small_ref, wide_ref, small_out, wide_out, sem):
    copies = [
        pltpu.make_async_copy(source, target, sem.at[slot])
        for slot, (source, target) in enumerate(((wide_ref, wide_out), (small_ref, small_out)))
    ]
    for copy in copies:
        copy.start()
    for copy in copies:
        copy.wait()


def placed_copy(small, wide):
    any_spec = pl.BlockSpec(memory_space=pl.ANY)
    vmem_spec = pl.BlockSpec(memory_space=pltpu.VMEM)
    return pl.pallas_call(
        place_kernel,
        out_shape=(
            jax.ShapeDtypeStruct(small.shape, small.dtype),
            jax.ShapeDtypeStruct(wide.shape, wide.dtype),
        ),
        in_specs=[vmem_spec] * 2,
        out_specs=(any_spec, any_spec),
        scratch_shapes=[pltpu.SemaphoreType.DMA((2,))],
    )(*(pltpu.with_memory_space_constraint(value, pltpu.VMEM) for value in (small, wide)))


def per_device(conv_input, gate_value, out_grad, long_filter, skip_bias, short_weight):
    channels, block_len = conv_input.shape
    taps = short_weight.shape[1]
    shards = lax.axis_size("ctx")
    any_spec = pl.BlockSpec(memory_space=pl.ANY)
    vmem_spec = pl.BlockSpec(memory_space=pltpu.VMEM)
    results = pl.pallas_call(
        functools.partial(gather_kernel, shards),
        out_shape=(
            pltpu.VMEM((channels, block_len), jnp.bfloat16),
            pltpu.VMEM((channels, block_len), jnp.float32),
        ),
        in_specs=[any_spec] * 6,
        out_specs=(vmem_spec, vmem_spec),
        scratch_shapes=[
            pltpu.VMEM((4, channels, LANES), jnp.bfloat16),
            pltpu.VMEM((1, channels), jnp.float32),
            pltpu.VMEM((taps, channels), jnp.float32),
            pltpu.VMEM((shards + 1, channels, LANES), jnp.bfloat16),
            pltpu.VMEM((shards + PAD, 2 * channels, LANES), jnp.bfloat16),
            pltpu.VMEM((channels // GROUP, LANES, LANES), jnp.bfloat16),
            pltpu.VMEM((channels // GROUP, 2 * GROUP * GROUP, LANES), jnp.float32),
            pltpu.VMEM((taps - 1, channels, LANES), jnp.float32),
            pltpu.SemaphoreType.DMA((2,)),
            pltpu.SemaphoreType.DMA,
            pltpu.SemaphoreType.DMA(((shards + 1) // 2,)),
            pltpu.SemaphoreType.DMA(((shards + 1) // 2,)),
            pltpu.SemaphoreType.REGULAR((shards // 2,)),
        ],
        compiler_params=pltpu.CompilerParams(
            collective_id=0,
            has_side_effects=True,
        ),
    )(
        conv_input,
        gate_value,
        out_grad,
        long_filter,
        skip_bias.reshape(1, channels),
        short_weight.T,
    )
    return placed_copy(*results)


def solution(mesh):
    placed = (
        P("ch", "ctx"),
        P("ch", "ctx"),
        P("ch", "ctx"),
        P("ch", "ctx"),
        P("ch"),
        P("ch", None),
    )
    return jax.shard_map(
        per_device,
        mesh=mesh,
        in_specs=placed,
        out_specs=(P("ch", "ctx"), P("ch", "ctx")),
        check_vma=False,
    )
```

```python
import functools
import math

import jax
import jax.numpy as jnp
from jax import lax
from jax.experimental import pallas as pl
from jax.experimental.pallas import tpu as pltpu
from jax.sharding import PartitionSpec as P

LANES = 128
GROUP = 8
EARLY = 3
PAD = 4


def gather_kernel(
    shards,
    input_ref,
    gate_ref,
    grad_ref,
    filter_ref,
    skip_ref,
    short_ref,
    input_grad_ref,
    filter_grad_ref,
    local,
    skip_row,
    short_rows,
    grads,
    pairs,
    rolled,
    sums,
    halo,
    load_sem,
    send_sem,
    grad_recv,
    pair_recv,
    entered,
):
    me = lax.axis_index("ctx")
    channels = local.shape[1]
    taps = short_rows.shape[0]
    groups = channels // GROUP
    bands = [slice(group * GROUP, (group + 1) * GROUP) for group in range(groups)]

    for slot, source in enumerate((gate_ref, grad_ref, filter_ref, input_ref)):
        pltpu.make_async_copy(source, local.at[slot], load_sem.at[slot // 2]).start()
    skip_load = pltpu.make_async_copy(skip_ref, skip_row, load_sem.at[0])
    short_load = pltpu.make_async_copy(short_ref, short_rows, load_sem.at[1])
    barrier = pltpu.get_barrier_semaphore()

    @pl.loop(me + 1, shards)
    def _(peer):
        pl.semaphore_signal(
            barrier, inc=1, device_id={"ctx": peer}, device_id_type=pl.DeviceIdType.MESH
        )

    @pl.when(me > 0)
    def _():
        pl.semaphore_wait(barrier, me)

    def party(peer):
        return (peer + 1) // 2

    @pl.loop(0, jnp.minimum(me, shards - me))
    def _(peer):
        pl.semaphore_signal(
            entered.at[party(me) - 1],
            inc=1,
            device_id={"ctx": peer},
            device_id_type=pl.DeviceIdType.MESH,
        )

    grads[shards] = jnp.zeros((channels, LANES), jnp.bfloat16)
    for spare in range(PAD):
        pairs[spare] = jnp.zeros((2 * channels, LANES), jnp.bfloat16)
    sums[...] = jnp.zeros_like(sums)
    halo[...] = jnp.zeros_like(halo)

    def parity(device):
        return lax.rem(shards - device, 2)

    def slot(step, target):
        last = (shards - target + parity(target)) // 2 - 2
        return jnp.minimum(step, jnp.maximum(last, 0))

    def grad_copy(source, target):
        return pltpu.make_async_remote_copy(
            src_ref=grads.at[source],
            dst_ref=grads.at[source],
            send_sem=send_sem,
            recv_sem=grad_recv.at[slot((source - target - 1 + parity(target)) // 2, target)],
            device_id={"ctx": target},
            device_id_type=pl.DeviceIdType.MESH,
        )

    def pair_copy(source, target):
        return pltpu.make_async_remote_copy(
            src_ref=pairs.at[source + PAD],
            dst_ref=pairs.at[source + PAD],
            send_sem=send_sem,
            recv_sem=pair_recv.at[slot((source + parity(target)) // 2, target)],
            device_id={"ctx": target},
            device_id_type=pl.DeviceIdType.MESH,
        )

    def wait_loads(half):
        blocks = local.at[pl.ds(2 * half, 2)]
        pltpu.make_async_copy(blocks, blocks, load_sem.at[half]).wait()

    wait_loads(0)
    grads[me] = (local[0].astype(jnp.float32) * local[1].astype(jnp.float32)).astype(jnp.bfloat16)

    @pl.when(me > 0)
    def _():
        grad_copy(me, 0).start()

    wait_loads(1)
    taken = [local[slot].astype(jnp.float32) for slot in (2, 3)]
    pairs[me + PAD] = jnp.concatenate(
        [source[band] for band in bands for source in taken], axis=0
    ).astype(jnp.bfloat16)

    @pl.when(me > 0)
    def _():
        pair_copy(me, 0).start()

    @pl.loop(1, me)
    def _(peer):
        grad_copy(me, peer).start()

        @pl.when(peer < shards - me)
        def _():
            pair_copy(me, peer).start()

    skip_load.start()
    short_load.start()
    lane_row = lax.broadcasted_iota(jnp.int32, (channels, LANES), 1)
    lane = lax.broadcasted_iota(jnp.int32, (GROUP, LANES), 1)
    row = lax.broadcasted_iota(jnp.int32, (GROUP, LANES), 0)
    diagonal = lane % GROUP == GROUP - 1 - row
    lane_pair = lax.broadcasted_iota(jnp.int32, (2 * channels, LANES), 1)
    span = lax.broadcasted_iota(jnp.int32, (LANES, LANES), 0) // GROUP * GROUP
    within = span + lax.broadcasted_iota(jnp.int32, (LANES, LANES), 1) < LANES

    def upside_down(value):
        value = pltpu.roll(value, 4, 0)
        value = jnp.where(row & 2 > 0, pltpu.roll(value, 2, 0), pltpu.roll(value, 6, 0))
        return jnp.where(row & 1 > 0, pltpu.roll(value, 1, 0), pltpu.roll(value, 7, 0))

    def coarse_shifts(grad):
        blocks = []
        for band in bands:
            flipped = upside_down(grad[band])
            turns = [flipped] + [
                pltpu.roll(flipped, LANES - shift, 1) for shift in range(GROUP, LANES, GROUP)
            ]
            blocks.append(jnp.concatenate(turns, axis=0).astype(jnp.bfloat16))
        return blocks

    def fine_shifts(pair, before):
        return [pair] + [
            pltpu.roll(jnp.where(lane_pair >= LANES - shift, before, pair), shift, 1)
            for shift in range(1, GROUP)
        ]

    def filter_rows(pair):
        wide_pair = pair.astype(jnp.float32)
        return jnp.concatenate(
            [wide_pair[2 * GROUP * group :][:GROUP] for group in range(groups)], axis=0
        )

    count = shards - me
    odd = parity(me)
    units = (count + odd) // 2

    def wait_for(buffer, start, size, sem):
        blocks = buffer.at[pl.ds(start, size)]
        pltpu.make_async_copy(blocks, blocks, sem).wait()

    def wait_grads(unit):
        lag = 2 * unit - odd + 1

        @pl.when(lag > 0)
        def _():
            wait_for(grads, me + lag, 2, grad_recv.at[unit])

        @pl.when(lag == 0)
        def _():
            wait_for(grads, me + lag + 1, 1, grad_recv.at[unit])

    last_grads = jnp.minimum(count - 1, 3)
    last_pairs = jnp.minimum(count, 4)
    last_pairs -= jnp.where(jnp.logical_and(me >= count - last_pairs, me < count), 1, 0)

    def wait_last(buffer, end, size, sems):
        for blocks in range(1, 5):

            @pl.when(size == blocks)
            def _():
                wait_for(buffer, end - blocks, blocks, sems.at[jnp.maximum(units - 2, 0)])

    def wait_pairs(unit):
        lag = 2 * unit - odd
        sem = pair_recv.at[unit]
        first = jnp.logical_and(lag >= 0, lag != me)
        second = jnp.logical_and(lag >= -1, lag + 1 != me)

        @pl.when(jnp.logical_and(first, second))
        def _():
            wait_for(pairs, lag + PAD, 2, sem)

        @pl.when(jnp.logical_and(first, jnp.logical_not(second)))
        def _():
            wait_for(pairs, lag + PAD, 1, sem)

        @pl.when(jnp.logical_and(jnp.logical_not(first), second))
        def _():
            wait_for(pairs, lag + PAD + 1, 1, sem)

    def products(unit, final):
        lag = 2 * unit - odd
        width = 4 if final else 2
        if final:
            wait_last(grads, shards, last_grads, grad_recv)
        else:
            wait_grads(unit)
        known = []
        for ahead in range(1, width + (not final)):
            at = lag + ahead
            grad = grads[jnp.maximum(me + at, 0)].astype(jnp.float32)
            known.append(jnp.where(at < 0, 0.0, grad) if final else grad)
        turns = [None] + [coarse_shifts(grad) for grad in known]
        if final:
            wait_last(pairs, count + PAD, last_pairs, pair_recv)
        else:
            wait_pairs(unit)
        blocks = [pairs[lag + PAD + ahead] for ahead in range(-1, width)]
        rows = [fine_shifts(new, old) for old, new in zip(blocks, blocks[1:])]
        found = []
        for group in range(groups):
            stack = [rolled[group]] + [turn[group] for turn in turns[1:]]
            if final:
                stack.append(jnp.zeros_like(stack[0]))
            hankel = jnp.concatenate(
                [jnp.where(within, old, new) for old, new in zip(stack, stack[1:])], axis=1
            )
            at = slice(2 * GROUP * group, 2 * GROUP * (group + 1))
            weights = jnp.concatenate(
                [jnp.concatenate([part[at] for part in parts], axis=0) for parts in rows],
                axis=1,
            )
            found.append(
                lax.dot_general(
                    weights,
                    hankel,
                    (((1,), (1,)), ((), ())),
                    preferred_element_type=jnp.float32,
                )
            )
            if not final:
                rolled[group] = stack[-1]
        for tap in range(taps - 1):
            more = None
            for grad, parts in zip(known, rows):
                term = grad * filter_rows(parts[tap])
                more = term if more is None else more + term
            halo[tap] += more
        return found

    own = grads[me].astype(jnp.float32)
    start = coarse_shifts(jnp.where(odd > 0, 0.0, own))
    for group in range(groups):
        rolled[group] = start[group]

    def push_up(wave):
        low = jnp.maximum(2 * wave - 1, me + 1)
        high = jnp.minimum(2 * wave + 1, shards - me)

        @pl.when(low < high)
        def _():
            pl.semaphore_wait(entered.at[wave - 1], high - low)

            @pl.loop(low, high)
            def _(peer):
                pair_copy(me, peer).start()

    nearest = party(me + 1)

    @pl.loop(nearest, nearest + EARLY)
    def _(wave):
        push_up(wave)

    skip_load.wait()
    short_load.wait()
    wide = skip_row.shape[1]
    eye = lax.broadcasted_iota(jnp.int32, (channels, wide), 0) == lax.broadcasted_iota(
        jnp.int32, (channels, wide), 1
    )

    def column(value):
        return jnp.sum(jnp.where(eye, value, 0.0), axis=1, keepdims=True)

    skip = column(skip_row[...])
    short = [column(short_rows[tap : tap + 1, :]) for tap in range(taps)]

    def step(unit, carry):
        for group, found in enumerate(products(unit, False)):
            sums[group] += found
        push_up(nearest + EARLY + unit)
        return carry

    lax.fori_loop(0, units - 2, step, 0)

    def rounded(value):
        return value.astype(jnp.bfloat16).astype(jnp.float32)

    direct = [
        skip * (own if tap == 0 else pltpu.roll(own, LANES - tap, 1)) for tap in range(taps)
    ]
    sent = shards - me - jnp.where(2 * me < shards, 1, 0)

    @pl.loop(0, me)
    def _(peer):
        grad_copy(me, peer).wait_send()

    @pl.loop(1, sent)
    def _(peer):
        pair_copy(me, lax.rem(me + 1, shards)).wait_send()

    totals = [sums[group] + found for group, found in enumerate(products(units - 2, True))]
    ahead_grad = grads[me + 1].astype(jnp.float32)
    edge = [
        rounded(jnp.sum(halo[tap], axis=1, keepdims=True) + skip * ahead_grad[:, tap : tap + 1])
        for tap in range(taps - 1)
    ]

    def folded(group, which):
        parts = []
        for shift in range(GROUP):
            at = (2 * shift + which) * GROUP
            part = jnp.where(diagonal, totals[group][at : at + GROUP], 0.0)
            parts.append(part if shift == 0 else pltpu.roll(part, shift, 1))
        while len(parts) > 1:
            parts = [left + right for left, right in zip(parts[::2], parts[1::2])]
        return parts[0]

    def straight(values, ahead):
        return jnp.concatenate(
            [
                pltpu.roll(value, LANES - GROUP + 1 - ahead, 1, stride=1, stride_axis=0)
                for value in values
            ],
            axis=0,
        )

    middles = [folded(group, 0) for group in range(groups)]
    total = None
    for tap in range(taps):
        moved = rounded(straight(middles, tap) + direct[tap])
        for reach in range(tap):
            moved = jnp.where(lane_row == LANES - tap + reach, edge[reach], moved)
        total = short[tap] * moved if total is None else total + short[tap] * moved
    input_grad_ref[...] = total.astype(jnp.bfloat16)
    scale = 1.0 / math.sqrt(shards * LANES)
    filter_grad_ref[...] = scale * straight([folded(group, 1) for group in range(groups)], 0)

    @pl.when(sent > 0)
    def _():
        pair_copy(me, lax.rem(me + 1, shards)).wait_send()


def place_kernel(small_ref, wide_ref, small_out, wide_out, sem):
    copies = [
        pltpu.make_async_copy(source, target, sem.at[slot])
        for slot, (source, target) in enumerate(((wide_ref, wide_out), (small_ref, small_out)))
    ]
    for copy in copies:
        copy.start()
    for copy in copies:
        copy.wait()


def placed_copy(small, wide):
    any_spec = pl.BlockSpec(memory_space=pl.ANY)
    vmem_spec = pl.BlockSpec(memory_space=pltpu.VMEM)
    return pl.pallas_call(
        place_kernel,
        out_shape=(
            jax.ShapeDtypeStruct(small.shape, small.dtype),
            jax.ShapeDtypeStruct(wide.shape, wide.dtype),
        ),
        in_specs=[vmem_spec] * 2,
        out_specs=(any_spec, any_spec),
        scratch_shapes=[pltpu.SemaphoreType.DMA((2,))],
    )(*(pltpu.with_memory_space_constraint(value, pltpu.VMEM) for value in (small, wide)))


def per_device(conv_input, gate_value, out_grad, long_filter, skip_bias, short_weight):
    channels, block_len = conv_input.shape
    taps = short_weight.shape[1]
    shards = lax.axis_size("ctx")
    any_spec = pl.BlockSpec(memory_space=pl.ANY)
    vmem_spec = pl.BlockSpec(memory_space=pltpu.VMEM)
    results = pl.pallas_call(
        functools.partial(gather_kernel, shards),
        out_shape=(
            pltpu.VMEM((channels, block_len), jnp.bfloat16),
            pltpu.VMEM((channels, block_len), jnp.float32),
        ),
        in_specs=[any_spec] * 6,
        out_specs=(vmem_spec, vmem_spec),
        scratch_shapes=[
            pltpu.VMEM((4, channels, LANES), jnp.bfloat16),
            pltpu.VMEM((1, channels), jnp.float32),
            pltpu.VMEM((taps, channels), jnp.float32),
            pltpu.VMEM((shards + 1, channels, LANES), jnp.bfloat16),
            pltpu.VMEM((shards + PAD, 2 * channels, LANES), jnp.bfloat16),
            pltpu.VMEM((channels // GROUP, LANES, LANES), jnp.bfloat16),
            pltpu.VMEM((channels // GROUP, 2 * GROUP * GROUP, LANES), jnp.float32),
            pltpu.VMEM((taps - 1, channels, LANES), jnp.float32),
            pltpu.SemaphoreType.DMA((2,)),
            pltpu.SemaphoreType.DMA,
            pltpu.SemaphoreType.DMA((max((shards + 1) // 2 - 1, 1),)),
            pltpu.SemaphoreType.DMA((max((shards + 1) // 2 - 1, 1),)),
            pltpu.SemaphoreType.REGULAR((shards // 2,)),
        ],
        compiler_params=pltpu.CompilerParams(
            collective_id=0,
            has_side_effects=True,
        ),
    )(
        conv_input,
        gate_value,
        out_grad,
        long_filter,
        skip_bias.reshape(1, channels),
        short_weight.T,
    )
    return placed_copy(*results)


def solution(mesh):
    placed = (
        P("ch", "ctx"),
        P("ch", "ctx"),
        P("ch", "ctx"),
        P("ch", "ctx"),
        P("ch"),
        P("ch", None),
    )
    return jax.shard_map(
        per_device,
        mesh=mesh,
        in_specs=placed,
        out_specs=(P("ch", "ctx"), P("ch", "ctx")),
        check_vma=False,
    )
```

```python
import functools
import math

import jax
import jax.numpy as jnp
from jax import lax
from jax.experimental import pallas as pl
from jax.experimental.pallas import tpu as pltpu
from jax.sharding import PartitionSpec as P

LANES = 128
GROUP = 8
EARLY = 3
PAD = 4


def gather_kernel(
    shards,
    input_ref,
    gate_ref,
    grad_ref,
    filter_ref,
    skip_ref,
    short_ref,
    input_grad_ref,
    filter_grad_ref,
    local,
    skip_row,
    short_rows,
    grads,
    pairs,
    rolled,
    sums,
    halo,
    load_sem,
    send_sem,
    grad_recv,
    pair_recv,
    entered,
):
    me = lax.axis_index("ctx")
    channels = local.shape[1]
    taps = short_rows.shape[0]
    groups = channels // GROUP
    bands = [slice(group * GROUP, (group + 1) * GROUP) for group in range(groups)]

    for slot, source in enumerate((gate_ref, grad_ref, filter_ref, input_ref)):
        sem = send_sem if slot < 2 else load_sem
        pltpu.make_async_copy(source, local.at[slot], sem).start()
    skip_load = pltpu.make_async_copy(skip_ref, skip_row, load_sem)
    short_load = pltpu.make_async_copy(short_ref, short_rows, load_sem)
    barrier = pltpu.get_barrier_semaphore()

    @pl.loop(me + 1, shards)
    def _(peer):
        pl.semaphore_signal(
            barrier, inc=1, device_id={"ctx": peer}, device_id_type=pl.DeviceIdType.MESH
        )

    @pl.when(me > 0)
    def _():
        pl.semaphore_wait(barrier, me)

    def party(peer):
        return (peer + 1) // 2

    @pl.loop(0, jnp.minimum(me, shards - me))
    def _(peer):
        pl.semaphore_signal(
            entered.at[party(me) - 1],
            inc=1,
            device_id={"ctx": peer},
            device_id_type=pl.DeviceIdType.MESH,
        )

    grads[shards] = jnp.zeros((channels, LANES), jnp.bfloat16)
    for spare in range(PAD):
        pairs[spare] = jnp.zeros((2 * channels, LANES), jnp.bfloat16)
    sums[...] = jnp.zeros_like(sums)
    halo[...] = jnp.zeros_like(halo)

    def parity(device):
        return lax.rem(shards - device, 2)

    def slot(step, target):
        last = (shards - target + parity(target)) // 2 - 2
        return jnp.minimum(step, jnp.maximum(last, 0))

    def grad_copy(source, target):
        return pltpu.make_async_remote_copy(
            src_ref=grads.at[source],
            dst_ref=grads.at[source],
            send_sem=send_sem,
            recv_sem=grad_recv.at[slot((source - target - 1 + parity(target)) // 2, target)],
            device_id={"ctx": target},
            device_id_type=pl.DeviceIdType.MESH,
        )

    def pair_copy(source, target):
        return pltpu.make_async_remote_copy(
            src_ref=pairs.at[source + PAD],
            dst_ref=pairs.at[source + PAD],
            send_sem=send_sem,
            recv_sem=pair_recv.at[slot((source + parity(target)) // 2, target)],
            device_id={"ctx": target},
            device_id_type=pl.DeviceIdType.MESH,
        )

    def wait_loads(half):
        blocks = local.at[pl.ds(2 * half, 2)]
        pltpu.make_async_copy(blocks, blocks, load_sem if half else send_sem).wait()

    wait_loads(0)
    grads[me] = (local[0].astype(jnp.float32) * local[1].astype(jnp.float32)).astype(jnp.bfloat16)

    @pl.when(me > 0)
    def _():
        grad_copy(me, 0).start()

    wait_loads(1)
    taken = [local[slot].astype(jnp.float32) for slot in (2, 3)]
    pairs[me + PAD] = jnp.concatenate(
        [source[band] for band in bands for source in taken], axis=0
    ).astype(jnp.bfloat16)

    @pl.when(me > 0)
    def _():
        pair_copy(me, 0).start()

    @pl.loop(1, me)
    def _(peer):
        grad_copy(me, peer).start()

        @pl.when(peer < shards - me)
        def _():
            pair_copy(me, peer).start()

    skip_load.start()
    lane_row = lax.broadcasted_iota(jnp.int32, (channels, LANES), 1)
    lane = lax.broadcasted_iota(jnp.int32, (GROUP, LANES), 1)
    row = lax.broadcasted_iota(jnp.int32, (GROUP, LANES), 0)
    diagonal = lane % GROUP == GROUP - 1 - row
    lane_pair = lax.broadcasted_iota(jnp.int32, (2 * channels, LANES), 1)
    span = lax.broadcasted_iota(jnp.int32, (LANES, LANES), 0) // GROUP * GROUP
    within = span + lax.broadcasted_iota(jnp.int32, (LANES, LANES), 1) < LANES

    def upside_down(value):
        value = pltpu.roll(value, 4, 0)
        value = jnp.where(row & 2 > 0, pltpu.roll(value, 2, 0), pltpu.roll(value, 6, 0))
        return jnp.where(row & 1 > 0, pltpu.roll(value, 1, 0), pltpu.roll(value, 7, 0))

    def coarse_shifts(grad):
        blocks = []
        for band in bands:
            flipped = upside_down(grad[band])
            turns = [flipped] + [
                pltpu.roll(flipped, LANES - shift, 1) for shift in range(GROUP, LANES, GROUP)
            ]
            blocks.append(jnp.concatenate(turns, axis=0).astype(jnp.bfloat16))
        return blocks

    def fine_shifts(pair, before):
        return [pair] + [
            pltpu.roll(jnp.where(lane_pair >= LANES - shift, before, pair), shift, 1)
            for shift in range(1, GROUP)
        ]

    def filter_rows(pair):
        wide_pair = pair.astype(jnp.float32)
        return jnp.concatenate(
            [wide_pair[2 * GROUP * group :][:GROUP] for group in range(groups)], axis=0
        )

    count = shards - me
    odd = parity(me)
    units = (count + odd) // 2

    def wait_for(buffer, start, size, sem):
        blocks = buffer.at[pl.ds(start, size)]
        pltpu.make_async_copy(blocks, blocks, sem).wait()

    def wait_grads(unit):
        lag = 2 * unit - odd + 1

        @pl.when(lag > 0)
        def _():
            wait_for(grads, me + lag, 2, grad_recv.at[unit])

        @pl.when(lag == 0)
        def _():
            wait_for(grads, me + lag + 1, 1, grad_recv.at[unit])

    last_grads = jnp.minimum(count - 1, 3)
    last_pairs = jnp.minimum(count, 4)
    last_pairs -= jnp.where(jnp.logical_and(me >= count - last_pairs, me < count), 1, 0)

    def wait_last(buffer, end, size, sems):
        for blocks in range(1, 5):

            @pl.when(size == blocks)
            def _():
                wait_for(buffer, end - blocks, blocks, sems.at[jnp.maximum(units - 2, 0)])

    def wait_pairs(unit):
        lag = 2 * unit - odd
        sem = pair_recv.at[unit]
        first = jnp.logical_and(lag >= 0, lag != me)
        second = jnp.logical_and(lag >= -1, lag + 1 != me)

        @pl.when(jnp.logical_and(first, second))
        def _():
            wait_for(pairs, lag + PAD, 2, sem)

        @pl.when(jnp.logical_and(first, jnp.logical_not(second)))
        def _():
            wait_for(pairs, lag + PAD, 1, sem)

        @pl.when(jnp.logical_and(jnp.logical_not(first), second))
        def _():
            wait_for(pairs, lag + PAD + 1, 1, sem)

    def products(unit, final):
        lag = 2 * unit - odd
        width = 4 if final else 2
        if final:
            wait_last(grads, shards, last_grads, grad_recv)
        else:
            wait_grads(unit)
        known = []
        for ahead in range(1, width + (not final)):
            at = lag + ahead
            grad = grads[jnp.maximum(me + at, 0)].astype(jnp.float32)
            known.append(jnp.where(at < 0, 0.0, grad) if final else grad)
        turns = [None] + [coarse_shifts(grad) for grad in known]
        if final:
            wait_last(pairs, count + PAD, last_pairs, pair_recv)
        else:
            wait_pairs(unit)
        blocks = [pairs[lag + PAD + ahead] for ahead in range(-1, width)]
        rows = [fine_shifts(new, old) for old, new in zip(blocks, blocks[1:])]
        found = []
        for group in range(groups):
            stack = [rolled[group]] + [turn[group] for turn in turns[1:]]
            if final:
                stack.append(jnp.zeros_like(stack[0]))
            hankel = jnp.concatenate(
                [jnp.where(within, old, new) for old, new in zip(stack, stack[1:])], axis=1
            )
            at = slice(2 * GROUP * group, 2 * GROUP * (group + 1))
            weights = jnp.concatenate(
                [jnp.concatenate([part[at] for part in parts], axis=0) for parts in rows],
                axis=1,
            )
            found.append(
                lax.dot_general(
                    weights,
                    hankel,
                    (((1,), (1,)), ((), ())),
                    preferred_element_type=jnp.float32,
                )
            )
            if not final:
                rolled[group] = stack[-1]
        for tap in range(taps - 1):
            more = None
            for grad, parts in zip(known, rows):
                term = grad * filter_rows(parts[tap])
                more = term if more is None else more + term
            halo[tap] += more
        return found

    own = grads[me].astype(jnp.float32)
    start = coarse_shifts(jnp.where(odd > 0, 0.0, own))
    for group in range(groups):
        rolled[group] = start[group]

    skip_load.wait()
    short_load.start()

    def push_up(wave):
        low = jnp.maximum(2 * wave - 1, me + 1)
        high = jnp.minimum(2 * wave + 1, shards - me)

        @pl.when(low < high)
        def _():
            pl.semaphore_wait(entered.at[wave - 1], high - low)

            @pl.loop(low, high)
            def _(peer):
                pair_copy(me, peer).start()

    nearest = party(me + 1)

    @pl.loop(nearest, nearest + EARLY)
    def _(wave):
        push_up(wave)

    short_load.wait()
    wide = skip_row.shape[1]
    eye = lax.broadcasted_iota(jnp.int32, (channels, wide), 0) == lax.broadcasted_iota(
        jnp.int32, (channels, wide), 1
    )

    def column(value):
        return jnp.sum(jnp.where(eye, value, 0.0), axis=1, keepdims=True)

    skip = column(skip_row[...])
    short = [column(short_rows[tap : tap + 1, :]) for tap in range(taps)]

    def step(unit, carry):
        for group, found in enumerate(products(unit, False)):
            sums[group] += found
        push_up(nearest + EARLY + unit)
        return carry

    lax.fori_loop(0, units - 2, step, 0)

    def rounded(value):
        return value.astype(jnp.bfloat16).astype(jnp.float32)

    direct = [
        skip * (own if tap == 0 else pltpu.roll(own, LANES - tap, 1)) for tap in range(taps)
    ]
    sent = shards - me - jnp.where(2 * me < shards, 1, 0)

    @pl.loop(0, me)
    def _(peer):
        grad_copy(me, peer).wait_send()

    @pl.loop(1, sent)
    def _(peer):
        pair_copy(me, lax.rem(me + 1, shards)).wait_send()

    totals = [sums[group] + found for group, found in enumerate(products(units - 2, True))]
    ahead_grad = grads[me + 1].astype(jnp.float32)
    edge = [
        rounded(jnp.sum(halo[tap], axis=1, keepdims=True) + skip * ahead_grad[:, tap : tap + 1])
        for tap in range(taps - 1)
    ]

    def folded(group, which):
        parts = []
        for shift in range(GROUP):
            at = (2 * shift + which) * GROUP
            part = jnp.where(diagonal, totals[group][at : at + GROUP], 0.0)
            parts.append(part if shift == 0 else pltpu.roll(part, shift, 1))
        while len(parts) > 1:
            parts = [left + right for left, right in zip(parts[::2], parts[1::2])]
        return parts[0]

    def straight(values, ahead):
        return jnp.concatenate(
            [
                pltpu.roll(value, LANES - GROUP + 1 - ahead, 1, stride=1, stride_axis=0)
                for value in values
            ],
            axis=0,
        )

    middles = [folded(group, 0) for group in range(groups)]
    total = None
    for tap in range(taps):
        moved = rounded(straight(middles, tap) + direct[tap])
        for reach in range(tap):
            moved = jnp.where(lane_row == LANES - tap + reach, edge[reach], moved)
        total = short[tap] * moved if total is None else total + short[tap] * moved
    input_grad_ref[...] = total.astype(jnp.bfloat16)
    scale = 1.0 / math.sqrt(shards * LANES)
    filter_grad_ref[...] = scale * straight([folded(group, 1) for group in range(groups)], 0)

    @pl.when(sent > 0)
    def _():
        pair_copy(me, lax.rem(me + 1, shards)).wait_send()


def place_kernel(small_ref, wide_ref, small_out, wide_out, sem):
    copies = [
        pltpu.make_async_copy(source, target, sem.at[slot])
        for slot, (source, target) in enumerate(((wide_ref, wide_out), (small_ref, small_out)))
    ]
    for copy in copies:
        copy.start()
    for copy in copies:
        copy.wait()


def placed_copy(small, wide):
    any_spec = pl.BlockSpec(memory_space=pl.ANY)
    vmem_spec = pl.BlockSpec(memory_space=pltpu.VMEM)
    return pl.pallas_call(
        place_kernel,
        out_shape=(
            jax.ShapeDtypeStruct(small.shape, small.dtype),
            jax.ShapeDtypeStruct(wide.shape, wide.dtype),
        ),
        in_specs=[vmem_spec] * 2,
        out_specs=(any_spec, any_spec),
        scratch_shapes=[pltpu.SemaphoreType.DMA((2,))],
    )(*(pltpu.with_memory_space_constraint(value, pltpu.VMEM) for value in (small, wide)))


def per_device(conv_input, gate_value, out_grad, long_filter, skip_bias, short_weight):
    channels, block_len = conv_input.shape
    taps = short_weight.shape[1]
    shards = lax.axis_size("ctx")
    any_spec = pl.BlockSpec(memory_space=pl.ANY)
    vmem_spec = pl.BlockSpec(memory_space=pltpu.VMEM)
    results = pl.pallas_call(
        functools.partial(gather_kernel, shards),
        out_shape=(
            pltpu.VMEM((channels, block_len), jnp.bfloat16),
            pltpu.VMEM((channels, block_len), jnp.float32),
        ),
        in_specs=[any_spec] * 6,
        out_specs=(vmem_spec, vmem_spec),
        scratch_shapes=[
            pltpu.VMEM((4, channels, LANES), jnp.bfloat16),
            pltpu.VMEM((1, channels), jnp.float32),
            pltpu.VMEM((taps, channels), jnp.float32),
            pltpu.VMEM((shards + 1, channels, LANES), jnp.bfloat16),
            pltpu.VMEM((shards + PAD, 2 * channels, LANES), jnp.bfloat16),
            pltpu.VMEM((channels // GROUP, LANES, LANES), jnp.bfloat16),
            pltpu.VMEM((channels // GROUP, 2 * GROUP * GROUP, LANES), jnp.float32),
            pltpu.VMEM((taps - 1, channels, LANES), jnp.float32),
            pltpu.SemaphoreType.DMA,
            pltpu.SemaphoreType.DMA,
            pltpu.SemaphoreType.DMA((max((shards + 1) // 2 - 1, 1),)),
            pltpu.SemaphoreType.DMA((max((shards + 1) // 2 - 1, 1),)),
            pltpu.SemaphoreType.REGULAR((shards // 2,)),
        ],
        compiler_params=pltpu.CompilerParams(
            collective_id=0,
            has_side_effects=True,
        ),
    )(
        conv_input,
        gate_value,
        out_grad,
        long_filter,
        skip_bias.reshape(1, channels),
        short_weight.T,
    )
    return placed_copy(*results)


def solution(mesh):
    placed = (
        P("ch", "ctx"),
        P("ch", "ctx"),
        P("ch", "ctx"),
        P("ch", "ctx"),
        P("ch"),
        P("ch", None),
    )
    return jax.shard_map(
        per_device,
        mesh=mesh,
        in_specs=placed,
        out_specs=(P("ch", "ctx"), P("ch", "ctx")),
        check_vma=False,
    )
```
